256 devices in a mesh: layer: 2 (over core), ex: 128 (over z, y, x).
Axes of the slice: x: 4, y: 4, z: 8, core: 2. Of those that a mesh axis runs over, the one named last changes fastest.
Arguments:
- train_sketch: bfloat16 [12, 65536, 256], P('layer', 'ex')
- val_sketch: bfloat16 [12, 4096, 256], P('layer', 'ex')
- first_moment: float32 [12, 256], P('layer'), may hold values from -0.6 to 0.6
- second_moment: float32 [12, 256], P('layer'), may hold values from 0.01 to 1
- train_pair: int32 [65536], P('ex'), may hold values from 0 to 15
- val_pair: int32 [4096], P('ex'), may hold values from 0 to 15
- block_mask: int32 [16, 16], replicated, may hold values 0 or 1
Outputs:
- scores: bfloat16 [32768, 2, 4096], P('ex', 'layer')
The draws below stay inside these ranges and needn't reach their ends.
All inputs are finite; a program needn't handle non-finite values.
Results may differ from the reference program's by a relative error of at most 0.0058.
Values may be sent and summed in bfloat16 or wider, within the bound.
No kernel may reach another device: no remote copies, remote signals or barrier semaphores. Data moves between devices by JAX's collectives and lax.ppermute only.
A program may use at most 128 MiB of HBM per device.

```python
import math
import jax
import jax.numpy as jnp
import numpy as np
from jax import lax

K = 256
PAIRS = 16
ROW_DEV = 256
L = 12
TR_EX = 512
NTRAIN = 65536
NVAL = 4096
N_LAYER = 2
N_EX = 128


def sketch_draw(key, layers, rows, width):
    ramp = 1.0 + 2.0 * jnp.arange(layers, dtype=jnp.float32) / max(layers - 1, 1)
    values = jax.random.normal(key, (layers, rows, width), jnp.float32)
    return values * ramp[:, None, None]


def draw_train_sketch(key, part):
    return sketch_draw(jax.random.fold_in(key, 11), L, NTRAIN, K).astype(jnp.bfloat16)


def draw_val_sketch(key, part):
    return sketch_draw(jax.random.fold_in(key, 23), L, NVAL, K).astype(jnp.bfloat16)


def touch_ends(result, key, least, largest):
    longest = result.shape.index(max(result.shape))
    spots = []
    for shift in (0, 1):
        where = [jax.random.randint(jax.random.fold_in(key, axis), (), 0, length) for axis, length in enumerate(result.shape)]
        where[longest] = (where[longest] + shift) % result.shape[longest]
        spots.append(tuple(where))
    return result.at[spots[0]].set(least).at[spots[1]].set(largest)


def level_of(key, extent, cuts, low, top_value):
    def one(dim, shards_of):
        draws = jax.random.uniform(jax.random.fold_in(jax.random.fold_in(key, 6), dim), (shards_of,), jnp.float32, low / len(cuts), top_value / len(cuts))
        return jnp.repeat(jnp.exp(draws), extent[dim] // shards_of).reshape((-1,) + (1,) * (len(extent) - dim - 1))

    factor_of = one(*cuts[0])
    for cut in cuts[1:]:
        factor_of = factor_of * one(*cut)
    return factor_of


def cumulative_ranks(number_of, lean):
    weights = [(1 << 20) // math.isqrt(standing ** lean) + 1 for standing in range(1, number_of + 1)]
    spread = 1 + sum(weights) // (1 << 30)
    return np.cumsum(np.array([max(1, weight // spread) for weight in weights]))


def ranked(own_key, dims, count, skew):
    grid = cumulative_ranks(count, skew)
    pick = jax.random.randint(jax.random.fold_in(own_key, 1), dims, 0, int(grid[count - 1]))
    grade = jnp.searchsorted(jnp.asarray(grid, jnp.int32), pick, side="right")
    return jax.random.permutation(jax.random.fold_in(own_key, 2), count)[grade].astype(jnp.int32)


def scatter_about(key, dims, scale, reach, pieces=(), kind=jnp.bfloat16):
    loudness = level_of(key, dims, pieces, -0.22, 0.18) if pieces else 1.0
    values = jax.random.normal(key, dims, jnp.float32) * scale * loudness
    return jnp.minimum(jnp.maximum(values, -reach), reach).astype(kind)


def setup_inputs(seed: int = 0) -> dict:
    seeds = jax.random.split(jax.random.key(seed), 8)
    train_sketch = draw_train_sketch(jax.random.fold_in(seeds[7], 71), 0)
    val_sketch = draw_val_sketch(jax.random.fold_in(seeds[7], 71), 0)
    first_moment = scatter_about(seeds[2], (L, K), 0.1, 0.6, ((0, 2),), jnp.float32)
    second_moment = jnp.clip(jnp.exp(math.log(1.0) - 4.6051702 * jax.random.uniform(seeds[3], (L, K), jnp.float32) ** level_of(seeds[3], (L, K), ((0, 2),), -0.2, 0.2)), 0.01, 1.0)
    train_pair = touch_ends(ranked(seeds[4], (NTRAIN,), PAIRS, 2), jax.random.fold_in(seeds[4], 3), 0, PAIRS - 1).astype(jnp.int32)
    val_pair = touch_ends(ranked(seeds[5], (NVAL,), PAIRS, 1), jax.random.fold_in(seeds[5], 3), 0, PAIRS - 1).astype(jnp.int32)
    block_mask = touch_ends((jax.random.randint(seeds[6], (PAIRS, PAIRS), 0, 2) < 1).astype(jnp.int32), jax.random.fold_in(seeds[6], 1), 0, 1)
    return dict(train_sketch=train_sketch, val_sketch=val_sketch, first_moment=first_moment, second_moment=second_moment, train_pair=train_pair, val_pair=val_pair, block_mask=block_mask)


def precondition(grad, first_moment, second_moment):
    return (0.9 * first_moment[:, None, :] + 0.1 * grad) / (jnp.sqrt(0.999 * second_moment[:, None, :] + 0.001 * grad * grad) + 1e-08)

def reference(train_sketch, val_sketch, first_moment, second_moment, train_pair, val_pair, block_mask):
    scale_factor = float(L * K) ** 0.25
    val_float = val_sketch.astype(jnp.float32)
    val_sq = lax.optimization_barrier(jnp.sum(val_float * val_float, axis=(0, 2)))
    unit_val = (val_float * (scale_factor * lax.rsqrt(val_sq + 1e-06))[None, :, None]).astype(jnp.bfloat16)
    val_table = block_mask[:, val_pair].astype(jnp.float32)

    def one_block(index):
        start = (index * TR_EX).astype(jnp.int32)
        grad = lax.dynamic_slice_in_dim(train_sketch, start, TR_EX, 1).astype(jnp.float32)
        pairs = lax.dynamic_slice_in_dim(train_pair, start, TR_EX, 0)
        pre = precondition(grad, first_moment, second_moment)
        train_sq = lax.optimization_barrier(jnp.sum(pre * pre, axis=(0, 2)))
        unit_train = (pre * (scale_factor * lax.rsqrt(train_sq + 1e-06))[None, :, None]).astype(jnp.bfloat16)
        raw = lax.dot_general(unit_train, unit_val, (((0, 2), (0, 2)), ((), ())), preferred_element_type=jnp.float32)
        masked = raw * val_table[pairs]
        return masked.astype(jnp.bfloat16).reshape(N_LAYER, ROW_DEV, NVAL).transpose(1, 0, 2)
    blocks = lax.map(one_block, jnp.arange(N_EX, dtype=jnp.int32))
    return blocks.reshape(N_EX * ROW_DEV, N_LAYER, NVAL)
```

```python
import jax
import jax.numpy as jnp
from jax import lax
from jax.experimental import pallas as pl
from jax.experimental.pallas import tpu as pltpu
from jax.sharding import PartitionSpec as P

SWAP = [(0, 1), (1, 0)]
NT = (((1,), (1,)), ((), ()))
NN = (((1,), (0,)), ((), ()))


def other(x):
    return lax.ppermute(x, "layer", SWAP)


def precondition(grad, first_moment, second_moment):
    return (0.9 * first_moment[:, None, :] + 0.1 * grad) / (
        jnp.sqrt(0.999 * second_moment[:, None, :] + 0.001 * grad * grad) + 1e-08
    )


def unit_rows(values, scale_factor):
    total_sq = jnp.sum(values * values, axis=(0, 2))
    return (values * (scale_factor * lax.rsqrt(total_sq + 1e-06))[None, :, None]).astype(
        jnp.bfloat16
    )


def pack_kernel(lay_ref, pair_ref, val_ref, recv_ref, out_ref):
    layers, both, width = val_ref.shape
    mine = both // 2
    first = pl.multiple_of(lay_ref[0] * mine, mine)
    pieces = [val_ref[l, pl.ds(first, mine), :] for l in range(layers)]
    pieces += [recv_ref[l] for l in range(layers)]
    pieces = [piece.astype(jnp.float32) for piece in pieces]
    total_sq = sum(jnp.sum(piece * piece, axis=1, keepdims=True) for piece in pieces)
    scale = float(2 * layers * width) ** 0.25 * lax.rsqrt(total_sq + 1e-06)
    for l, piece in enumerate(pieces):
        out_ref[:, l * width : (l + 1) * width] = (piece * scale).astype(out_ref.dtype)
    row = lax.broadcasted_iota(jnp.int32, (mine, 128), 0)
    label = jnp.zeros((mine, 128), jnp.int32)
    for r in range(mine):
        label = jnp.where(row == r, pair_ref[first + r], label)
    lane = lax.broadcasted_iota(jnp.int32, (mine, 128), 1)
    out_ref[:, 2 * layers * width :] = jnp.where(label == lane, 1.0, 0.0).astype(out_ref.dtype)


def pack(lay, val_pair, val_sketch, recv):
    layers, both, width = val_sketch.shape
    return pl.pallas_call(
        pack_kernel,
        grid_spec=pltpu.PrefetchScalarGridSpec(
            num_scalar_prefetch=2,
            grid=(1,),
            in_specs=[
                pl.BlockSpec(val_sketch.shape, lambda i, *s: (0, 0, 0)),
                pl.BlockSpec(recv.shape, lambda i, *s: (0, 0, 0)),
            ],
            out_specs=pl.BlockSpec((both // 2, 2 * layers * width + 128), lambda i, *s: (0, 0)),
        ),
        out_shape=jax.ShapeDtypeStruct((both // 2, 2 * layers * width + 128), jnp.bfloat16),
        name="pack",
    )(lay, val_pair, val_sketch, recv)


def score_kernel(lay_ref, a_ref, m_ref, b_ref, own_ref, oth_ref):
    layers, rows, width = a_ref.shape
    half = rows // 2
    depth = layers * width
    lay = lay_ref[0]
    for which, out_ref in ((lay, own_ref), (1 - lay, oth_ref)):
        part = pl.ds(pl.multiple_of(which * half, half), half)
        left = jnp.concatenate([a_ref[l, part, :] for l in range(layers)], axis=1)
        raw = lax.dot_general(
            left, b_ref[:, :depth], NT, preferred_element_type=jnp.float32
        )
        weight = lax.dot_general(
            m_ref[part, :], b_ref[:, depth:], NT, preferred_element_type=jnp.float32
        )
        out_ref[...] = (raw * weight).astype(out_ref.dtype)


def score(lay, a, row_mask, b, tile):
    layers, rows, width = a.shape
    cols, wide = b.shape
    shape = jax.ShapeDtypeStruct((rows // 2, cols), jnp.bfloat16)
    return pl.pallas_call(
        score_kernel,
        grid_spec=pltpu.PrefetchScalarGridSpec(
            num_scalar_prefetch=1,
            grid=(cols // tile,),
            in_specs=[
                pl.BlockSpec((layers, rows, width), lambda j, s: (0, 0, 0)),
                pl.BlockSpec(row_mask.shape, lambda j, s: (0, 0)),
                pl.BlockSpec((tile, wide), lambda j, s: (j, 0)),
            ],
            out_specs=[pl.BlockSpec((rows // 2, tile), lambda j, s: (0, j))] * 2,
        ),
        out_shape=[shape, shape],
        compiler_params=pltpu.CompilerParams(vmem_limit_bytes=48 << 20),
        name="score",
    )(lay, a, row_mask, b)


def place_kernel(own_ref, recv_ref, spread_ref, out_ref):
    both = jnp.concatenate([own_ref[...], recv_ref[...]], axis=1)
    out_ref[...] = lax.dot_general(
        both, spread_ref[...], NN, preferred_element_type=jnp.float32
    ).astype(out_ref.dtype)


def place(own, recv, spread, tile):
    rows, cols = own.shape
    return pl.pallas_call(
        place_kernel,
        grid=(cols // tile,),
        in_specs=[
            pl.BlockSpec((rows, tile), lambda j: (0, j)),
            pl.BlockSpec((rows, tile), lambda j: (0, j)),
            pl.BlockSpec((2 * tile, 2 * tile), lambda j: (0, 0)),
        ],
        out_specs=pl.BlockSpec((rows, 2 * tile), lambda j: (0, j)),
        out_shape=jax.ShapeDtypeStruct((rows, 2 * cols), jnp.bfloat16),
        name="place",
    )(own, recv, spread)


def local(train_sketch, val_sketch, first_moment, second_moment, train_pair, val_pair, block_mask):
    lay_dev, tr_ex, width = train_sketch.shape
    val_ex = val_sketch.shape[1]
    mine = val_ex // 2
    lay = lax.axis_index("layer")
    scale_factor = float(2 * lay_dev * width) ** 0.25
    pairs = block_mask.shape[0]
    labels = jnp.arange(128, dtype=jnp.int32)

    give = lax.dynamic_slice_in_dim(val_sketch, (1 - lay) * mine, mine, 1)
    payload = pack(lay[None], val_pair, val_sketch, other(give))
    everyone = lax.all_gather(payload, "ex", axis=0, tiled=True)

    train = jnp.concatenate([train_sketch, other(train_sketch)], axis=0)
    moments = jnp.stack([first_moment, second_moment])
    moments = jnp.concatenate([moments, other(moments)], axis=1)
    pre = precondition(train.astype(jnp.float32), moments[0], moments[1])
    unit_train = unit_rows(pre, scale_factor)
    train_onehot = (train_pair[:, None] == labels[None, :pairs]).astype(jnp.bfloat16)
    wide_mask = jnp.pad(block_mask.astype(jnp.bfloat16), ((0, 0), (0, 128 - pairs)))
    row_mask = jnp.dot(train_onehot, wide_mask, preferred_element_type=jnp.float32).astype(
        jnp.bfloat16
    )

    own, oth = score(lay[None], unit_train, row_mask, everyone, 256)
    recv = other(oth)
    tile = 128
    at = jnp.arange(tile, dtype=jnp.int32)
    base = (at // mine) * val_ex + at % mine
    target = jnp.concatenate([base + lay * mine, base + (1 - lay) * mine])
    spread = (target[:, None] == jnp.arange(2 * tile, dtype=jnp.int32)[None, :]).astype(
        jnp.bfloat16
    )
    return place(own, recv, spread, tile)[:, None, :]


def solution(mesh):
    placed = (
        P("layer", "ex", None),
        P("layer", "ex", None),
        P("layer", None),
        P("layer", None),
        P("ex"),
        P("ex"),
        P(),
    )
    return jax.shard_map(
        local, mesh=mesh, in_specs=placed, out_specs=P("ex", "layer", None), check_vma=False
    )
```

```python
import jax
import jax.numpy as jnp
from jax import lax
from jax.experimental import pallas as pl
from jax.experimental.pallas import tpu as pltpu
from jax.sharding import PartitionSpec as P

SWAP = [(0, 1), (1, 0)]
NT = (((1,), (1,)), ((), ()))
NN = (((1,), (0,)), ((), ()))


def other(x):
    return lax.ppermute(x, "layer", SWAP)


def precondition(grad, first_moment, second_moment):
    return (0.9 * first_moment[:, None, :] + 0.1 * grad) / (
        jnp.sqrt(0.999 * second_moment[:, None, :] + 0.001 * grad * grad) + 1e-08
    )


def unit_rows(values, scale_factor):
    total_sq = jnp.sum(values * values, axis=(0, 2))
    return (values * (scale_factor * lax.rsqrt(total_sq + 1e-06))[None, :, None]).astype(
        jnp.bfloat16
    )


def pack_kernel(lay_ref, pair_ref, val_ref, recv_ref, out_ref):
    layers, both, width = val_ref.shape
    mine = both // 2
    first = pl.multiple_of(lay_ref[0] * mine, mine)
    pieces = [val_ref[l, pl.ds(first, mine), :] for l in range(layers)]
    pieces += [recv_ref[l] for l in range(layers)]
    pieces = [piece.astype(jnp.float32) for piece in pieces]
    total_sq = sum(jnp.sum(piece * piece, axis=1, keepdims=True) for piece in pieces)
    scale = float(2 * layers * width) ** 0.25 * lax.rsqrt(total_sq + 1e-06)
    for l, piece in enumerate(pieces):
        out_ref[:, l * width : (l + 1) * width] = (piece * scale).astype(out_ref.dtype)
    row = lax.broadcasted_iota(jnp.int32, (mine, 128), 0)
    label = jnp.zeros((mine, 128), jnp.int32)
    for r in range(mine):
        label = jnp.where(row == r, pair_ref[first + r], label)
    lane = lax.broadcasted_iota(jnp.int32, (mine, 128), 1)
    out_ref[:, 2 * layers * width :] = jnp.where(label == lane, 1.0, 0.0).astype(out_ref.dtype)


def pack(lay, val_pair, val_sketch, recv):
    layers, both, width = val_sketch.shape
    return pl.pallas_call(
        pack_kernel,
        grid_spec=pltpu.PrefetchScalarGridSpec(
            num_scalar_prefetch=2,
            grid=(1,),
            in_specs=[
                pl.BlockSpec(val_sketch.shape, lambda i, *s: (0, 0, 0)),
                pl.BlockSpec(recv.shape, lambda i, *s: (0, 0, 0)),
            ],
            out_specs=pl.BlockSpec((both // 2, 2 * layers * width + 128), lambda i, *s: (0, 0)),
        ),
        out_shape=jax.ShapeDtypeStruct((both // 2, 2 * layers * width + 128), jnp.bfloat16),
        name="pack",
    )(lay, val_pair, val_sketch, recv)


SIZE = {"z": 8, "y": 4, "x": 4}
RING8 = (0, -1, 1, -2, 2, -3, 3, 4)
RING4 = (0, -1, 1, 2)
C_COLUMNS = 1152


def shifted(axis, step):
    chips = []
    for chip in range(128):
        at = {"z": chip // 16, "y": chip // 4 % 4, "x": chip % 4}
        at[axis] = (at[axis] + step) % SIZE[axis]
        chips.append(at["z"] * 16 + at["y"] * 4 + at["x"])
    return chips


def send(block, axes, step):
    pairs = [
        (128 * core + chip, 128 * core + there)
        for core in (0, 1)
        for chip, there in enumerate(shifted(axes[core], step))
    ]
    return lax.ppermute(block, ("layer", "ex"), pairs)


def around8(block):
    half = block.shape[0] // 2
    up = down = block
    found = [block]
    for _ in range(3):
        up, down = send(up, "zz", 1), send(down, "zz", -1)
        found += [up, down]
    return found, (send(up[:half], "zz", 1), send(down[half:], "zz", -1))


def straight4(block, axes):
    return jnp.concatenate([block] + [send(block, axes, step) for step in (1, -1, 2)], axis=0)


def around4(block, axes):
    half = block.shape[0] // 2
    up, down = send(block, axes, 1), send(block, axes, -1)
    return up, down, send(up[:half], axes, 1), send(down[half:], axes, -1)


def both_halves(s_ref, a_ref, m_ref, d, c, own_ref, oth_ref, cols):
    layers, rows, width = a_ref.shape
    half = rows // 2
    depth = d.shape[1]
    lay = s_ref[0]
    for which, out_ref in ((lay, own_ref), (1 - lay, oth_ref)):
        part = pl.ds(pl.multiple_of(which * half, half), half)
        left = jnp.concatenate([a_ref[l, part, :] for l in range(layers)], axis=1)
        raw = lax.dot_general(left[:, :depth], d, NT, preferred_element_type=jnp.float32)
        raw += lax.dot_general(left[:, depth:], c[:, :-128], NT, preferred_element_type=jnp.float32)
        weight = lax.dot_general(
            m_ref[part, :], c[:, -128:], NT, preferred_element_type=jnp.float32
        )
        out_ref[:, cols] = (raw * weight).astype(out_ref.dtype)


def early_kernel(s_ref, a_ref, m_ref, *refs):
    d_refs, c_refs = refs[:3], refs[3:12]
    own_ref, oth_ref, late_ref, c_all = refs[12:]
    step = pl.program_id(0)

    for k in range(7):

        @pl.when(step == k)
        def _():
            c_all[...] = c_refs[k][...]

    @pl.when(step == 7)
    def _():
        near = c_refs[7].shape[0]
        c_all[:near] = c_refs[7][...]
        c_all[near:] = c_refs[8][...]

    d = jnp.concatenate([ref[...].reshape(-1, ref.shape[-1]) for ref in d_refs], axis=0)
    cut = d.shape[0]
    both_halves(s_ref, a_ref, m_ref, d, c_all[:cut], own_ref, oth_ref, slice(0, cut))
    for ref in (own_ref, oth_ref):
        ref[:, cut:] = jnp.zeros((ref.shape[0], ref.shape[1] - cut), ref.dtype)
    late_ref[...] = c_all[cut:]


def whole(block):
    return pl.BlockSpec(block.shape, lambda *_: (0,) * block.ndim, pipeline_mode=pl.Buffered(1))


def early_score(lay, a, row_mask, d_blocks, c_blocks):
    layers, rows, width = a.shape
    cols = c_blocks[0].shape[0]
    c_wide = c_blocks[0].shape[1]
    late = cols // 4
    shape = jax.ShapeDtypeStruct((rows // 2, 8 * cols), jnp.bfloat16)

    def d_spec(block):
        return pl.BlockSpec((block.shape[0], None) + block.shape[2:], lambda j, s: (0, j, 0, 0))

    return pl.pallas_call(
        early_kernel,
        grid_spec=pltpu.PrefetchScalarGridSpec(
            num_scalar_prefetch=1,
            grid=(8,),
            in_specs=[whole(a), whole(row_mask)]
            + [d_spec(block) for block in d_blocks]
            + [whole(block) for block in c_blocks],
            out_specs=[pl.BlockSpec((rows // 2, cols), lambda j, s: (0, j))] * 2
            + [pl.BlockSpec((late, c_wide), lambda j, s: (j, 0))],
            scratch_shapes=[pltpu.VMEM((cols, c_wide), jnp.bfloat16)],
        ),
        out_shape=[shape, shape, jax.ShapeDtypeStruct((8 * late, c_wide), jnp.bfloat16)],
        compiler_params=pltpu.CompilerParams(vmem_limit_bytes=56 << 20),
        cost_estimate=pl.CostEstimate(
            flops=2 * rows * 6 * cols * layers * width, bytes_accessed=30 << 20, transcendentals=0
        ),
        name="early_score",
    )(lay, a, row_mask, *d_blocks, *c_blocks)


def late_kernel(s_ref, a_ref, m_ref, near_ref, far_ref, c_ref, own_ref, oth_ref):
    pieces = []
    for j in range(near_ref.shape[1]):
        for ref in (near_ref, far_ref):
            pieces += [ref[i, j] for i in range(ref.shape[0])]
    d = jnp.concatenate(pieces, axis=0)
    both_halves(s_ref, a_ref, m_ref, d, c_ref[...], own_ref, oth_ref, slice(None))


def late_score(lay, a, row_mask, near, far, c):
    layers, rows, width = a.shape
    shape = jax.ShapeDtypeStruct((rows // 2, c.shape[0]), jnp.bfloat16)
    smem = pl.BlockSpec(memory_space=pltpu.SMEM)
    vmem = pl.BlockSpec(memory_space=pltpu.VMEM)
    return pl.pallas_call(
        late_kernel,
        in_specs=[smem] + [vmem] * 5,
        out_specs=[vmem] * 2,
        out_shape=[shape, shape],
        compiler_params=pltpu.CompilerParams(vmem_limit_bytes=56 << 20),
        name="late_score",
    )(lay, a, row_mask, near, far, c)


def place_kernel(depth_ref, own_ref, recv_ref, own2_ref, recv2_ref, spread_ref, out_ref):
    tile = own_ref.shape[1] // 8
    for j in range(8):
        cols = slice(j * tile, (j + 1) * tile)
        pair = slice(j // 2 * 128, (j // 2 + 1) * 128)
        both = jnp.concatenate(
            [own_ref[:, cols], recv_ref[:, cols], own2_ref[:, pair], recv2_ref[:, pair]], axis=1
        )
        into = pl.ds(pl.multiple_of(depth_ref[j] * 2 * tile, 2 * tile), 2 * tile)
        out_ref[:, into] = lax.dot_general(
            both, spread_ref[j % 2], NN, preferred_element_type=jnp.float32
        ).astype(out_ref.dtype)


def place(depth, own, recv, own2, recv2, spread):
    rows, cols = own.shape
    vmem = pl.BlockSpec(memory_space=pltpu.VMEM)
    return pl.pallas_call(
        place_kernel,
        in_specs=[pl.BlockSpec(memory_space=pltpu.SMEM)] + [vmem] * 5,
        out_specs=vmem,
        out_shape=jax.ShapeDtypeStruct((rows, 2 * cols), jnp.bfloat16),
        compiler_params=pltpu.CompilerParams(vmem_limit_bytes=56 << 20),
        name="place",
    )(depth, own, recv, own2, recv2, spread)


def columns(core, chip, mine):
    at = jnp.arange(256, dtype=jnp.int32)
    ring = jnp.array(RING4, jnp.int32)
    first = ring[at // mine % 4]
    second = ring[at // (4 * mine)]
    along_x = jnp.where(core == 0, first, second)
    along_y = jnp.where(core == 0, second, first)
    x = (chip % 4 + along_x) % 4
    y = (chip // 4 % 4 + along_y) % 4
    return (y * 4 + x) * (2 * mine) + core * mine + at % mine


def spread_targets(lay, chip, mine):
    sides = []
    for core in (lay, 1 - lay):
        target = columns(core, chip, mine)
        cut = 12 * mine
        early = jnp.where(jnp.arange(256) < cut, target, -1)
        none = jnp.full((4 * mine,), -1, jnp.int32)
        late = target[cut:]
        sides.append((early, jnp.concatenate([late, none]), jnp.concatenate([none, late])))
    (early, even, odd), (early_there, even_there, odd_there) = sides
    return jnp.stack(
        [
            jnp.concatenate([early, early_there, even, even_there]),
            jnp.concatenate([early, early_there, odd, odd_there]),
        ]
    )


def local(train_sketch, val_sketch, first_moment, second_moment, train_pair, val_pair, block_mask):
    lay_dev, tr_ex, width = train_sketch.shape
    val_ex = val_sketch.shape[1]
    mine = val_ex // 2
    lay = lax.axis_index("layer")
    scale_factor = float(2 * lay_dev * width) ** 0.25
    pairs = block_mask.shape[0]
    labels = jnp.arange(128, dtype=jnp.int32)

    give = lax.dynamic_slice_in_dim(val_sketch, (1 - lay) * mine, mine, 1)
    payload = pack(lay[None], val_pair, val_sketch, other(give))
    train = other(train_sketch)
    moments = jnp.stack([first_moment, second_moment])
    moments_there = other(moments)
    payload, train, moments_there = lax.optimization_barrier((payload, train, moments_there))
    train = jnp.concatenate([train_sketch, train], axis=0)
    moments = jnp.concatenate([moments, moments_there], axis=1)

    cut = payload.shape[1] - C_COLUMNS
    stacks, ends = around8(payload[:, :cut])
    stack = jnp.concatenate(stacks + list(ends), axis=0)
    slab = straight4(stack, "xy")
    d_blocks = [
        block.reshape(-1, 8, mine, cut) for block in (slab,) + around4(slab, "yx")
    ]
    plane = straight4(straight4(payload[:, cut:], "xy"), "yx")
    planes, ends = around8(plane)
    c_blocks = planes + list(ends)

    pre = precondition(train.astype(jnp.float32), moments[0], moments[1])
    unit_train = unit_rows(pre, scale_factor)
    train_onehot = (train_pair[:, None] == labels[None, :pairs]).astype(jnp.bfloat16)
    wide_mask = jnp.pad(block_mask.astype(jnp.bfloat16), ((0, 0), (0, 128 - pairs)))
    row_mask = jnp.dot(train_onehot, wide_mask, preferred_element_type=jnp.float32).astype(
        jnp.bfloat16
    )

    chip = lax.axis_index("ex")
    depth = (chip // 16 + jnp.array(RING8, jnp.int32)) % 8
    own, oth, late = early_score(lay[None], unit_train, row_mask, d_blocks[:3], c_blocks)
    recv = other(oth)
    own2, oth2 = late_score(lay[None], unit_train, row_mask, *d_blocks[3:], late)
    recv2 = other(oth2)
    target = spread_targets(lay, chip, mine)
    spread = (target[:, :, None] == jnp.arange(512, dtype=jnp.int32)).astype(jnp.bfloat16)
    return place(depth, own, recv, own2, recv2, spread)[:, None, :]


def solution(mesh):
    placed = (
        P("layer", "ex", None),
        P("layer", "ex", None),
        P("layer", None),
        P("layer", None),
        P("ex"),
        P("ex"),
        P(),
    )
    return jax.shard_map(
        local, mesh=mesh, in_specs=placed, out_specs=P("ex", "layer", None), check_vma=False
    )
```
